32 devices in a mesh: groups: 2 (over y), segment: 8 (over z, x), space: 2 (over core).
Axes of the slice: x: 2, y: 2, z: 4, core: 2. Of those that a mesh axis runs over, the one named last changes fastest.
Arguments:
- patches: bfloat16 [16, 256, 1536], P(('groups', 'segment'), 'space'), parts along dimension 0, may hold values from -120 to 120
- positions: int32 [16], P(('groups', 'segment')), parts along dimension 0, may hold values from 0 to 1
- timesteps: int32 [16], P(('groups', 'segment')), parts along dimension 0, may hold values from 0 to 1
- section_bounds: int32 [9], replicated, may hold values from 0 to 12, as said below
- tile_neighbours: int32 [4, 2], replicated, may hold values from 0 to 3, as said below
- modulation: bfloat16 [6, 12, 3, 1536], P('groups'), parts along dimension 0, may hold values from -9 to 9
- query_gain: float32 [12, 128], replicated, may hold values from 0.5 to 2
- stale_kv: bfloat16 [16, 2, 2, 512, 1536], P(('groups', 'segment'), None, None, 'space'), parts along dimension 0, may hold values from -70 to 70
Outputs:
- advanced: bfloat16 [16, 256, 1536], P(('groups', 'segment'), 'space'), parts along dimension 0
The draws below stay inside these ranges and needn't reach their ends.
There are 2 independent parts, one for each index of `groups`. The reference program is written for one: setup_inputs(seed, part) draws one part's arguments, and reference() takes and returns one part's arrays. A program takes and returns all parts, laid end to end along the dimension named above; an argument that names none is the same for every part. Nothing has to cross between parts.
Inputs may be any that keep to these rules, and one draw needn't show every extreme that they name: section_bounds[0] is 0 and section_bounds[8] is 12; section j holds layers section_bounds[j] to section_bounds[j+1] - 1, one or 2 of them, and some sections hold 2. `tile_neighbours`: tile g lies in time layer g // 2; row g names first a tile of its own time layer, then a tile of the other time layer.
All inputs are finite; a program needn't handle non-finite values.
Results may differ from the reference program's by a relative error of at most 0.0051.
Values may be sent and summed in bfloat16 or wider, within the bound.
No kernel may reach another device: no remote copies, remote signals or barrier semaphores. Data moves between devices by JAX's collectives and lax.ppermute only.
A program may use at most 64 MiB of HBM per device.

```python
import math
import jax
import jax.numpy as jnp
from jax import lax

HEADS = 12
HDIM = 128
D = 1536
TILE = 128
GH = 2
GW = 1
SLAB_DEV = 2
NT = 4
NB = 2
PIPE = 8
LMAX = 2
LAYERS = 12
STEPS = 3
TICKS = 2
LANES = 1
PTOK = 256
PATCHES = 8
N_SEGMENT = 8
N_SPACE = 2


def draw_patches(key, part):
    drawn = jnp.clip(jax.random.normal(jax.random.fold_in(key, 31), (PATCHES, PTOK, D), jnp.float32), -4.0, 4.0)
    return drawn.astype(jnp.bfloat16)


def draw_section_bounds(key, part):
    shuffled = jax.random.permutation(jax.random.fold_in(key, 41), PIPE)
    counts = 1 + (shuffled < LAYERS - PIPE).astype(jnp.int32)
    bounds = jnp.concatenate([jnp.zeros((1,), jnp.int32), jnp.cumsum(counts).astype(jnp.int32)])
    return bounds


def draw_tile_neighbours(key, part):
    tile_ids = jnp.arange(NT, dtype=jnp.int32)
    layer_of = tile_ids // SLAB_DEV
    own_tile = layer_of * SLAB_DEV + jax.random.randint(jax.random.fold_in(key, 51), (NT,), 0, SLAB_DEV)
    other_tile = (1 - layer_of) * SLAB_DEV + jax.random.randint(jax.random.fold_in(key, 52), (NT,), 0, SLAB_DEV)
    return jnp.stack([own_tile, other_tile], axis=1).astype(jnp.int32)


def draw_modulation(key, part):
    shape_rows = (STEPS, LAYERS, D)
    shift_rows = 0.5 * jnp.clip(jax.random.normal(jax.random.fold_in(key, 21), shape_rows, jnp.float32), -4.0, 4.0)
    scale_rows = 0.3 * jnp.clip(jax.random.normal(jax.random.fold_in(key, 22), shape_rows, jnp.float32), -4.0, 4.0)
    gate_rows = 0.8 * jnp.clip(jax.random.normal(jax.random.fold_in(key, 23), shape_rows, jnp.float32), -4.0, 4.0)
    return jnp.stack([shift_rows, scale_rows, gate_rows], axis=2).astype(jnp.bfloat16)


def draw_stale_kv(key, part):
    key_part = jax.random.fold_in(key, 11)
    value_part = jax.random.fold_in(key, 12)
    shape_tiles = (N_SEGMENT, LMAX, NT, TILE, D)
    key_rows = jnp.clip(jax.random.normal(key_part, shape_tiles, jnp.float32), -4.0, 4.0)
    value_rows = 2.0 * jnp.clip(jax.random.normal(value_part, shape_tiles, jnp.float32), -4.0, 4.0)
    stacked = jnp.stack([key_rows, value_rows], axis=2)
    return stacked.reshape(N_SEGMENT, LMAX, 2, NT * TILE, D).astype(jnp.bfloat16)


def set_ends(entries, rng, least, top_value):
    dims = entries.shape
    spot = [jax.random.randint(jax.random.fold_in(rng, axis), (), 0, dims[axis]) for axis in range(len(dims))]
    entries = entries.at[tuple(spot)].set(least)
    longest = dims.index(max(dims))
    spot[longest] = (spot[longest] + 1) % dims[longest]
    return entries.at[tuple(spot)].set(top_value)


def setup_inputs(seed: int = 0, part: int = 0) -> dict:
    key_list = jax.random.split(jax.random.key(seed), 9)
    part_splits = jax.random.split(jax.random.fold_in(key_list[8], part), 9)
    return {
        "patches": draw_patches(jax.random.fold_in(jax.random.fold_in(key_list[8], part), 71), part),
        "positions": set_ends(jax.random.randint(part_splits[1], (PATCHES,), 0, GH * GW), jax.random.fold_in(part_splits[1], 1), 0, (GH * GW) - 1).astype(jnp.int32),
        "timesteps": set_ends(jax.random.randint(part_splits[2], (PATCHES,), 0, STEPS - 1), jax.random.fold_in(part_splits[2], 1), 0, (STEPS - 1) - 1).astype(jnp.int32),
        "section_bounds": draw_section_bounds(jax.random.fold_in(key_list[8], 71), part),
        "tile_neighbours": draw_tile_neighbours(jax.random.fold_in(key_list[8], 71), part),
        "modulation": draw_modulation(jax.random.fold_in(jax.random.fold_in(key_list[8], part), 71), part),
        "query_gain": jnp.clip(jnp.exp(jax.random.uniform(key_list[6], (LAYERS, HDIM), jnp.float32, math.log(0.5), math.log(2.0))), 0.5, 2.0),
        "stale_kv": draw_stale_kv(jax.random.fold_in(jax.random.fold_in(key_list[8], part), 71), part),
    }


epsilon = 1e-06

def attend(stream, key_tiles, value_tiles, tile_choice, mod_rows, gain_row):
    batch_size = stream.shape[0]
    middle = lax.optimization_barrier(jnp.mean(stream, axis=-1, keepdims=True))
    centred = stream - middle
    spread = lax.optimization_barrier(jnp.mean(centred * centred, axis=-1, keepdims=True))
    normed = centred * lax.rsqrt(spread + epsilon)
    shifted = normed * (1.0 + mod_rows[:, 1:2, :]) + mod_rows[:, 0:1, :]
    heads_in = shifted.reshape(batch_size, TILE, HEADS, HDIM)
    head_rms = lax.optimization_barrier(jnp.mean(heads_in * heads_in, axis=-1, keepdims=True))
    queries = (heads_in * lax.rsqrt(head_rms + epsilon) * gain_row).astype(jnp.bfloat16)
    key_rows = key_tiles[tile_choice].reshape(batch_size, NB * TILE, HEADS, HDIM)
    value_rows = value_tiles[tile_choice].reshape(batch_size, NB * TILE, HEADS, HDIM)
    scores = jnp.einsum('bqhd,bkhd->bhqk', queries.astype(jnp.float32), key_rows.astype(jnp.float32)) * HDIM ** (-0.5)
    row_max = lax.optimization_barrier(jnp.max(scores, axis=-1, keepdims=True))
    powers = jnp.exp(scores - row_max)
    totals = lax.optimization_barrier(jnp.sum(powers, axis=-1))
    weights = powers.astype(jnp.bfloat16)
    blended = jnp.einsum('bhqk,bkhd->bqhd', weights.astype(jnp.float32), value_rows.astype(jnp.float32))
    blended = blended / jnp.transpose(totals, (0, 2, 1))[..., None]
    return stream + mod_rows[:, 2:3, :] * blended.reshape(batch_size, TILE, D)

def run_section(stream, kv_slab, section, pos_one, step_one, section_bounds, tile_neighbours, modulation, query_gain):
    first_layer = section_bounds[section]
    layer_count = section_bounds[section + 1] - first_layer
    tile_states = stream.astype(jnp.float32).reshape(LANES * N_SPACE, TILE, D)
    core_ids = jnp.tile(jnp.arange(N_SPACE, dtype=jnp.int32), LANES)
    item_pos = jnp.repeat(pos_one, N_SPACE)
    item_step = jnp.repeat(step_one, N_SPACE)
    query_tile = core_ids * SLAB_DEV + item_pos
    tile_choice = tile_neighbours[query_tile]
    for slot_index in range(LMAX):
        layer_now = jnp.minimum(first_layer + slot_index, LAYERS - 1)
        mod_rows = modulation[item_step, layer_now].astype(jnp.float32)
        gain_row = query_gain[layer_now]
        key_tiles = kv_slab[slot_index, 0].reshape(NT, TILE, D)
        value_tiles = kv_slab[slot_index, 1].reshape(NT, TILE, D)
        updated = attend(tile_states, key_tiles, value_tiles, tile_choice, mod_rows, gain_row)
        tile_states = jnp.where(slot_index < layer_count, updated, tile_states)
    return tile_states.reshape(LANES, PTOK, D).astype(jnp.bfloat16)

def reference(patches, positions, timesteps, section_bounds, tile_neighbours, modulation, query_gain, stale_kv):
    holding = patches.reshape(N_SEGMENT, LANES, PTOK, D)
    pos_table = positions.reshape(N_SEGMENT, LANES)
    step_table = timesteps.reshape(N_SEGMENT, LANES)
    devices = jnp.arange(N_SEGMENT, dtype=jnp.int32)
    sections = devices % PIPE
    for tick_index in range(TICKS):
        root = (devices - tick_index) % N_SEGMENT
        crossed = (root % PIPE + tick_index >= PIPE).astype(jnp.int32)
        step_rows = step_table[root] + crossed[:, None]
        pos_rows = pos_table[root]

        def one_device(packed):
            stream, kv_slab, section, pos_one, step_one = packed
            return run_section(stream, kv_slab, section, pos_one, step_one, section_bounds, tile_neighbours, modulation, query_gain)
        updated = lax.map(one_device, (holding, stale_kv, sections, pos_rows, step_rows))
        holding = jnp.roll(updated, 1, axis=0)
    return holding.reshape(PATCHES, PTOK, D)
```

```python
import functools
import math
import jax
import jax.numpy as jnp
from jax import lax
from jax.experimental import pallas as pl
from jax.experimental.pallas import tpu as pltpu
from jax.sharding import PartitionSpec as P

TICKS = 2
EPSILON = 1e-06


def from_behind(x, axis, by):
    devices = lax.axis_size(axis)
    return lax.ppermute(x, axis, [(i, (i + by) % devices) for i in range(devices)])


def section_kernel(
    tick,
    cycle_size,
    bounds_ref,
    neighbours_ref,
    position_ref,
    step_ref,
    patch_ref,
    modulation_ref,
    gain_ref,
    own_ref,
    other_ref,
    out_ref,
    state_ref,
    query_ref,
):
    width = patch_ref.shape[1]
    layers, head_dim = gain_ref.shape
    heads = width // head_dim
    slots = own_ref.shape[0]
    tile = head_dim
    tile = own_ref.shape[2] // (neighbours_ref.shape[1] // 2)
    slab = own_ref.shape[2] // tile
    pipe = bounds_ref.shape[0] - 1
    device = lax.axis_index("segment")
    space = lax.axis_index("space")
    section = lax.rem(device, pipe)
    root = lax.rem(device - tick + cycle_size, cycle_size)
    row = step_ref[0] + jnp.where(lax.rem(root, pipe) + tick >= pipe, 1, 0)
    first_layer = bounds_ref[section]
    layer_count = bounds_ref[section + 1] - first_layer
    query_tile = space * slab + position_ref[0]
    own_row = pl.multiple_of(lax.rem(neighbours_ref[0, query_tile], slab) * tile, tile)
    other_row = pl.multiple_of(lax.rem(neighbours_ref[1, query_tile], slab) * tile, tile)
    scale = head_dim ** -0.5 * math.log2(math.e)

    state_ref[...] = patch_ref[...].astype(jnp.float32)

    def layer(slot):
        layer_now = jnp.minimum(first_layer + slot, layers - 1)
        mods = modulation_ref[row, layer_now].astype(jnp.float32)
        gain = gain_ref[pl.ds(layer_now, 1), :]
        state = state_ref[...]
        middle = jnp.mean(state, axis=-1, keepdims=True)
        centred = state - middle
        spread = jnp.mean(centred * centred, axis=-1, keepdims=True)
        normed = centred * lax.rsqrt(spread + EPSILON)
        shifted = normed * (1.0 + mods[1:2, :]) + mods[0:1, :]
        for head in range(heads):
            cols = slice(head * head_dim, (head + 1) * head_dim)
            part = shifted[:, cols]
            power = jnp.mean(part * part, axis=-1, keepdims=True)
            query_ref[:, cols] = (part * lax.rsqrt(power + EPSILON) * gain).astype(jnp.bfloat16)
        for head in range(heads):
            cols = slice(head * head_dim, (head + 1) * head_dim)
            keys = jnp.concatenate(
                [own_ref[slot, 0, pl.ds(own_row, tile), cols], other_ref[slot, 0, pl.ds(other_row, tile), cols]]
            )
            values = jnp.concatenate(
                [own_ref[slot, 1, pl.ds(own_row, tile), cols], other_ref[slot, 1, pl.ds(other_row, tile), cols]]
            )
            scores = lax.dot_general(
                query_ref[:, cols], keys, (((1,), (1,)), ((), ())), preferred_element_type=jnp.float32
            )
            top = jnp.max(scores, axis=-1, keepdims=True)
            powers = jnp.exp2((scores - top) * scale)
            total = jnp.sum(powers, axis=-1, keepdims=True)
            blended = jnp.dot(powers.astype(jnp.bfloat16), values, preferred_element_type=jnp.float32)
            state_ref[:, cols] += mods[2:3, cols] * (blended / total)

    layer(0)
    for slot in range(1, slots):
        pl.when(layer_count > slot)(functools.partial(layer, slot))
    out_ref[...] = state_ref[...].astype(jnp.bfloat16)


def run_section(tick, cycle_size, patch, position, step, bounds, neighbours, modulation, gains, own, other):
    rows, width = patch.shape
    smem = pl.BlockSpec(memory_space=pltpu.SMEM)
    vmem = pl.BlockSpec(memory_space=pltpu.VMEM)
    pin = lambda x: pltpu.with_memory_space_constraint(x, pltpu.VMEM)
    return pl.pallas_call(
        functools.partial(section_kernel, tick, cycle_size),
        out_shape=jax.ShapeDtypeStruct((rows, width), jnp.bfloat16),
        in_specs=[smem] * 4 + [vmem] * 5,
        out_specs=vmem,
        scratch_shapes=[
            pltpu.VMEM((rows, width), jnp.float32),
            pltpu.VMEM((rows, width), jnp.bfloat16),
        ],
        compiler_params=pltpu.CompilerParams(vmem_limit_bytes=16 << 20),
        cost_estimate=pl.CostEstimate(flops=800_000_000, bytes_accessed=8_000_000, transcendentals=800_000),
        name="section",
    )(bounds, neighbours, position, step, patch, pin(modulation), pin(gains), pin(own), pin(other))


def per_device(
    patches, positions, timesteps, section_bounds, tile_neighbours, modulation, query_gain, stale_kv
):
    own = stale_kv[0]
    other = from_behind(own, "space", 1)
    cycle_size = lax.axis_size("segment")
    neighbours = tile_neighbours.T
    holding = patches[0]
    position, step = positions, timesteps
    for tick in range(TICKS):
        if tick > 0:
            position, step = from_behind((position, step), "segment", 1)
        holding = run_section(
            tick, cycle_size, holding, position, step, section_bounds, neighbours, modulation, query_gain, own, other
        )
        holding = from_behind(holding, "segment", 1)
    return holding[None]


def solution(mesh):
    placed = (
        P(("groups", "segment"), "space", None),
        P(("groups", "segment")),
        P(("groups", "segment")),
        P(),
        P(),
        P("groups", None, None, None),
        P(),
        P(("groups", "segment"), None, None, "space", None),
    )
    return jax.shard_map(
        per_device,
        mesh=mesh,
        in_specs=placed,
        out_specs=P(("groups", "segment"), "space", None),
        check_vma=False,
    )
```

```python
import functools
import math
import jax
import jax.numpy as jnp
from jax import lax
from jax.experimental import pallas as pl
from jax.experimental.pallas import tpu as pltpu
from jax.sharding import PartitionSpec as P

TICKS = 2
CHUNKS = 2
EPSILON = 1e-06
EXTRA = 8

SMEM = pl.BlockSpec(memory_space=pltpu.SMEM)
VMEM = pl.BlockSpec(memory_space=pltpu.VMEM)
ANY = pl.BlockSpec(memory_space=pl.ANY)


def from_behind(x, axis, by):
    devices = lax.axis_size(axis)
    return lax.ppermute(x, axis, [(i, (i + by) % devices) for i in range(devices)])


def pinned(x, space=pltpu.VMEM):
    return pltpu.with_memory_space_constraint(x, space)


def stage_kernel(
    bounds_hbm,
    neighbours_hbm,
    position_ref,
    step_ref,
    patch_ref,
    modulation_ref,
    gain_ref,
    own_ref,
    plan_ref,
    patch_out,
    modulation_out,
    gain_out,
    own_out,
    bounds_ref,
    neighbours_ref,
    sems,
):
    slots = own_ref.shape[0]
    small = [
        pltpu.make_async_copy(source, target, sems.at[3 + slots + i])
        for i, (source, target) in enumerate(
            [
                (bounds_hbm, bounds_ref),
                (neighbours_hbm, neighbours_ref),
            ]
        )
    ]
    copies = [
        pltpu.make_async_copy(patch_ref, patch_out, sems.at[0]),
        pltpu.make_async_copy(gain_ref, gain_out, sems.at[1]),
        pltpu.make_async_copy(own_ref, own_out, sems.at[2]),
    ]
    for copy in small + copies:
        copy.start()
    for copy in small:
        copy.wait()
    pipe = bounds_ref.shape[0] - 1
    layers = gain_ref.shape[0]
    device = lax.axis_index("segment")
    space = lax.axis_index("space")
    section = lax.rem(device, pipe)
    first_layer = bounds_ref[section]
    for slot in range(slots):
        layer_now = jnp.minimum(first_layer + slot, layers - 1)
        copy = pltpu.make_async_copy(modulation_ref.at[:, layer_now], modulation_out.at[slot], sems.at[3 + slot])
        copy.start()
        copies.append(copy)
    slab = neighbours_ref.shape[1] // 2
    plan_ref[0] = first_layer
    plan_ref[1] = bounds_ref[section + 1] - first_layer
    plan_ref[2] = position_ref[0]
    plan_ref[3] = step_ref[0]
    for place in range(slab):
        plan_ref[4 + place] = lax.rem(neighbours_ref[0, space * slab + place], slab)
        plan_ref[4 + slab + place] = lax.rem(neighbours_ref[1, space * slab + place], slab)
    for copy in copies:
        copy.wait()


def stage(bounds, neighbours, position, step, patch, modulation, gains, own):
    slots = own.shape[0]
    plan_size = 4 + neighbours.shape[1]
    return pl.pallas_call(
        stage_kernel,
        out_shape=(
            pltpu.SMEM((plan_size,), jnp.int32),
            pltpu.VMEM(patch.shape, patch.dtype),
            pltpu.VMEM((slots, modulation.shape[0]) + modulation.shape[2:], modulation.dtype),
            pltpu.VMEM(gains.shape, gains.dtype),
            pltpu.VMEM(own.shape, own.dtype),
        ),
        in_specs=[ANY] * 2 + [SMEM] * 2 + [ANY] * 4,
        out_specs=(SMEM, VMEM, VMEM, VMEM, VMEM),
        scratch_shapes=[pltpu.SMEM(x.shape, x.dtype) for x in (bounds, neighbours)]
        + [pltpu.SemaphoreType.DMA((5 + slots,))],
        compiler_params=pltpu.CompilerParams(vmem_limit_bytes=16 << 20),
        cost_estimate=pl.CostEstimate(flops=0, bytes_accessed=7_000_000, transcendentals=0),
        name="stage",
    )(
        pinned(bounds, pltpu.HBM),
        pinned(neighbours, pltpu.HBM),
        position,
        step,
        *(pinned(x, pltpu.HBM) for x in (patch, modulation, gains, own)),
    )


def section_kernel(
    tick,
    start,
    cycle_size,
    pipe,
    plan_ref,
    patch_ref,
    modulation_ref,
    gain_ref,
    own_ref,
    other_ref,
    out_ref,
    state_ref,
):
    rows, width = state_ref.shape
    layers, head_dim = gain_ref.shape
    heads = width // head_dim
    slots = own_ref.shape[0]
    slab = (plan_ref.shape[0] - 4) // 2
    tile = own_ref.shape[2] // slab
    device = lax.axis_index("segment")
    root = lax.rem(device - tick + cycle_size, cycle_size)
    if tick == 0:
        position = plan_ref[2]
        step = plan_ref[3]
    else:
        tail = patch_ref[heads * rows : heads * rows + EXTRA, :].astype(jnp.float32)
        lanes = lax.broadcasted_iota(jnp.int32, tail.shape, 1)
        position = jnp.max(jnp.where(lanes == 0, tail, 0.0)).astype(jnp.int32)
        step = jnp.max(jnp.where(lanes == 1, tail, 0.0)).astype(jnp.int32)
    row = step + jnp.where(lax.rem(root, pipe) + tick >= pipe, 1, 0)
    first_layer = plan_ref[0]
    layer_count = plan_ref[1]
    own_row = pl.multiple_of(plan_ref[4 + position] * tile, tile)
    other_row = pl.multiple_of(plan_ref[4 + slab + position] * tile, tile)
    scale = head_dim ** -0.5 * math.log2(math.e)

    for head in range(heads):
        cols = slice(head * head_dim, (head + 1) * head_dim)
        if tick == 0:
            state_ref[:, cols] = patch_ref[start : start + rows, cols].astype(jnp.float32)
        else:
            state_ref[:, cols] = patch_ref[head * rows : (head + 1) * rows, :].astype(jnp.float32)

    def layer(slot):
        layer_now = jnp.minimum(first_layer + slot, layers - 1)
        mods = modulation_ref[slot, row].astype(jnp.float32)
        gain = gain_ref[pl.ds(layer_now, 1), :]
        blocks = [slice(head * head_dim, (head + 1) * head_dim) for head in range(heads)]

        def tiles(kind, cols):
            return jnp.concatenate(
                [
                    own_ref[slot, kind, pl.ds(own_row, tile), cols],
                    other_ref[slot, kind, pl.ds(other_row, tile), cols],
                ]
            )

        state = [state_ref[:, cols] for cols in blocks]
        middle = jnp.sum(sum(state[1:], state[0]), axis=-1, keepdims=True) / width
        centred = [part - middle for part in state]
        squares = [part * part for part in centred]
        spread = jnp.sum(sum(squares[1:], squares[0]), axis=-1, keepdims=True) / width
        sharp = lax.rsqrt(spread + EPSILON)
        shifted = [
            part * sharp * (1.0 + mods[1:2, cols]) + mods[0:1, cols] for part, cols in zip(centred, blocks)
        ]
        powers = [jnp.mean(part * part, axis=-1, keepdims=True) for part in shifted]
        queries = [
            (part * lax.rsqrt(power + EPSILON) * gain).astype(jnp.bfloat16)
            for part, power in zip(shifted, powers)
        ]
        scores = [
            lax.dot_general(
                query, tiles(0, cols), (((1,), (1,)), ((), ())), preferred_element_type=jnp.float32
            )
            for query, cols in zip(queries, blocks)
        ]
        tops = [jnp.max(part, axis=-1, keepdims=True) for part in scores]
        weights = [jnp.exp2((part - top) * scale) for part, top in zip(scores, tops)]
        totals = [jnp.sum(part, axis=-1, keepdims=True) for part in weights]
        blended = [
            jnp.dot(part.astype(jnp.bfloat16), tiles(1, cols), preferred_element_type=jnp.float32)
            for part, cols in zip(weights, blocks)
        ]
        for part, blend, total, cols in zip(state, blended, totals, blocks):
            state_ref[:, cols] = part + mods[2:3, cols] * (blend / total)

    layer(0)
    for slot in range(1, slots):
        pl.when(layer_count > slot)(functools.partial(layer, slot))

    if tick == 0:
        for head in range(heads):
            cols = slice(head * head_dim, (head + 1) * head_dim)
            out_ref[head * rows : (head + 1) * rows, :] = state_ref[:, cols].astype(out_ref.dtype)
        lanes = lax.broadcasted_iota(jnp.int32, (EXTRA, head_dim), 1)
        tail = jnp.where(lanes == 0, position, jnp.where(lanes == 1, step, 0))
        out_ref[heads * rows : heads * rows + EXTRA, :] = tail.astype(jnp.float32).astype(out_ref.dtype)
    else:
        out_ref[...] = state_ref[...].astype(out_ref.dtype)


def run_section(tick, start, rows, cycle_size, pipe, width, plan, patch, modulation, gains, own, other):
    heads = width // gains.shape[1]
    shape = (heads * rows + EXTRA, gains.shape[1]) if tick == 0 else (rows, width)
    return pl.pallas_call(
        functools.partial(section_kernel, tick, start, cycle_size, pipe),
        out_shape=pltpu.VMEM(shape, jnp.bfloat16),
        in_specs=[SMEM] + [VMEM] * 5,
        out_specs=VMEM,
        scratch_shapes=[pltpu.VMEM((rows, width), jnp.float32)],
        compiler_params=pltpu.CompilerParams(vmem_limit_bytes=16 << 20),
        cost_estimate=pl.CostEstimate(flops=400_000_000, bytes_accessed=8_000_000, transcendentals=800_000),
        name=f"section_{tick}_{start}",
    )(plan, pinned(patch), pinned(modulation), pinned(gains), pinned(own), pinned(other))


def per_device(
    patches, positions, timesteps, section_bounds, tile_neighbours, modulation, query_gain, stale_kv
):
    own_hbm = stale_kv[0]
    other = from_behind(own_hbm, "space", 1)
    cycle_size = lax.axis_size("segment")
    pipe = section_bounds.shape[0] - 1
    tokens, width = patches.shape[1:]
    plan, patch, mods, gains, own = stage(
        section_bounds, tile_neighbours.T, positions, timesteps, patches[0], modulation, query_gain, own_hbm
    )
    rows = tokens // CHUNKS
    pieces = [patch] * CHUNKS
    for tick in range(TICKS):
        pieces = [
            from_behind(
                run_section(
                    tick, chunk * rows, rows, cycle_size, pipe, width, plan, piece, mods, gains, own, other
                ),
                "segment",
                1,
            )
            for chunk, piece in enumerate(pieces)
        ]
    return jnp.concatenate(pieces)[None]


def solution(mesh):
    placed = (
        P(("groups", "segment"), "space", None),
        P(("groups", "segment")),
        P(("groups", "segment")),
        P(),
        P(),
        P("groups", None, None, None),
        P(),
        P(("groups", "segment"), None, None, "space", None),
    )
    return jax.shard_map(
        per_device,
        mesh=mesh,
        in_specs=placed,
        out_specs=P(("groups", "segment"), "space", None),
        check_vma=False,
    )
```

```python
import functools
import math
import jax
import jax.numpy as jnp
from jax import lax
from jax.experimental import pallas as pl
from jax.experimental.pallas import tpu as pltpu
from jax.sharding import PartitionSpec as P

TICKS = 2
CHUNKS = 3
UNIT = 16
EPSILON = 1e-06
EXTRA = 8

SMEM = pl.BlockSpec(memory_space=pltpu.SMEM)
VMEM = pl.BlockSpec(memory_space=pltpu.VMEM)
ANY = pl.BlockSpec(memory_space=pl.ANY)


def from_behind(x, axis, by):
    devices = lax.axis_size(axis)
    return lax.ppermute(x, axis, [(i, (i + by) % devices) for i in range(devices)])


def pinned(x, space=pltpu.VMEM):
    return pltpu.with_memory_space_constraint(x, space)


def stage_kernel(
    bounds_hbm,
    neighbours_hbm,
    position_ref,
    step_ref,
    patch_ref,
    modulation_ref,
    gain_ref,
    own_ref,
    plan_ref,
    patch_out,
    modulation_out,
    gain_out,
    own_out,
    bounds_ref,
    neighbours_ref,
    sems,
):
    slots = own_ref.shape[0]
    small = [
        pltpu.make_async_copy(source, target, sems.at[3 + slots + i])
        for i, (source, target) in enumerate(
            [
                (bounds_hbm, bounds_ref),
                (neighbours_hbm, neighbours_ref),
            ]
        )
    ]
    copies = [
        pltpu.make_async_copy(patch_ref, patch_out, sems.at[0]),
        pltpu.make_async_copy(gain_ref, gain_out, sems.at[1]),
        pltpu.make_async_copy(own_ref, own_out, sems.at[2]),
    ]
    for copy in small + copies:
        copy.start()
    for copy in small:
        copy.wait()
    pipe = bounds_ref.shape[0] - 1
    layers = gain_ref.shape[0]
    device = lax.axis_index("segment")
    space = lax.axis_index("space")
    section = lax.rem(device, pipe)
    first_layer = bounds_ref[section]
    for slot in range(slots):
        layer_now = jnp.minimum(first_layer + slot, layers - 1)
        copy = pltpu.make_async_copy(modulation_ref.at[:, layer_now], modulation_out.at[slot], sems.at[3 + slot])
        copy.start()
        copies.append(copy)
    slab = neighbours_ref.shape[1] // 2
    plan_ref[0] = first_layer
    plan_ref[1] = bounds_ref[section + 1] - first_layer
    plan_ref[2] = position_ref[0]
    plan_ref[3] = step_ref[0]
    for place in range(slab):
        plan_ref[4 + place] = lax.rem(neighbours_ref[0, space * slab + place], slab)
        plan_ref[4 + slab + place] = lax.rem(neighbours_ref[1, space * slab + place], slab)
    for copy in copies:
        copy.wait()


def stage(bounds, neighbours, position, step, patch, modulation, gains, own):
    slots = own.shape[0]
    plan_size = 4 + neighbours.shape[1]
    return pl.pallas_call(
        stage_kernel,
        out_shape=(
            pltpu.SMEM((plan_size,), jnp.int32),
            pltpu.VMEM(patch.shape, patch.dtype),
            pltpu.VMEM((slots, modulation.shape[0]) + modulation.shape[2:], modulation.dtype),
            pltpu.VMEM(gains.shape, gains.dtype),
            pltpu.VMEM(own.shape, own.dtype),
        ),
        in_specs=[ANY] * 2 + [SMEM] * 2 + [ANY] * 4,
        out_specs=(SMEM, VMEM, VMEM, VMEM, VMEM),
        scratch_shapes=[pltpu.SMEM(x.shape, x.dtype) for x in (bounds, neighbours)]
        + [pltpu.SemaphoreType.DMA((5 + slots,))],
        compiler_params=pltpu.CompilerParams(vmem_limit_bytes=16 << 20),
        cost_estimate=pl.CostEstimate(flops=0, bytes_accessed=7_000_000, transcendentals=0),
        name="stage",
    )(
        pinned(bounds, pltpu.HBM),
        pinned(neighbours, pltpu.HBM),
        position,
        step,
        *(pinned(x, pltpu.HBM) for x in (patch, modulation, gains, own)),
    )


def section_kernel(
    tick,
    start,
    cycle_size,
    pipe,
    plan_ref,
    patch_ref,
    modulation_ref,
    gain_ref,
    own_ref,
    other_ref,
    out_ref,
    state_ref,
):
    rows, width = state_ref.shape
    layers, head_dim = gain_ref.shape
    heads = width // head_dim
    slots = own_ref.shape[0]
    slab = (plan_ref.shape[0] - 4) // 2
    tile = own_ref.shape[2] // slab
    device = lax.axis_index("segment")
    root = lax.rem(device - tick + cycle_size, cycle_size)
    if tick == 0:
        position = plan_ref[2]
        step = plan_ref[3]
    else:
        tail = patch_ref[heads * rows : heads * rows + EXTRA, :].astype(jnp.float32)
        lanes = lax.broadcasted_iota(jnp.int32, tail.shape, 1)
        position = jnp.max(jnp.where(lanes == 0, tail, 0.0)).astype(jnp.int32)
        step = jnp.max(jnp.where(lanes == 1, tail, 0.0)).astype(jnp.int32)
    row = step + jnp.where(lax.rem(root, pipe) + tick >= pipe, 1, 0)
    first_layer = plan_ref[0]
    layer_count = plan_ref[1]
    own_row = pl.multiple_of(plan_ref[4 + position] * tile, tile)
    other_row = pl.multiple_of(plan_ref[4 + slab + position] * tile, tile)
    scale = head_dim ** -0.5 * math.log2(math.e)

    for head in range(heads):
        cols = slice(head * head_dim, (head + 1) * head_dim)
        if tick == 0:
            state_ref[:, cols] = patch_ref[start : start + rows, cols].astype(jnp.float32)
        else:
            state_ref[:, cols] = patch_ref[head * rows : (head + 1) * rows, :].astype(jnp.float32)

    def layer(slot):
        layer_now = jnp.minimum(first_layer + slot, layers - 1)
        mods = modulation_ref[slot, row].astype(jnp.float32)
        gain = gain_ref[pl.ds(layer_now, 1), :]
        blocks = [slice(head * head_dim, (head + 1) * head_dim) for head in range(heads)]

        def tiles(kind, cols):
            return jnp.concatenate(
                [
                    own_ref[slot, kind, pl.ds(own_row, tile), cols],
                    other_ref[slot, kind, pl.ds(other_row, tile), cols],
                ]
            )

        state = [state_ref[:, cols] for cols in blocks]
        middle = jnp.sum(sum(state[1:], state[0]), axis=-1, keepdims=True) / width
        centred = [part - middle for part in state]
        squares = [part * part for part in centred]
        spread = jnp.sum(sum(squares[1:], squares[0]), axis=-1, keepdims=True) / width
        sharp = lax.rsqrt(spread + EPSILON)
        shifted = [
            part * sharp * (1.0 + mods[1:2, cols]) + mods[0:1, cols] for part, cols in zip(centred, blocks)
        ]
        powers = [jnp.mean(part * part, axis=-1, keepdims=True) for part in shifted]
        queries = [
            (part * lax.rsqrt(power + EPSILON) * gain).astype(jnp.bfloat16)
            for part, power in zip(shifted, powers)
        ]
        pairs = range(0, heads, 2)
        doubles = [slice(head * head_dim, (head + 2) * head_dim) for head in pairs]
        blank = jnp.zeros((rows, head_dim), jnp.bfloat16)
        paired = [
            jnp.concatenate(
                [
                    jnp.concatenate([queries[head], blank], axis=1),
                    jnp.concatenate([blank, queries[head + 1]], axis=1),
                ]
            )
            for head in pairs
        ]
        scores = [
            lax.dot_general(
                query, tiles(0, cols), (((1,), (1,)), ((), ())), preferred_element_type=jnp.float32
            )
            for query, cols in zip(paired, doubles)
        ]
        tops = [jnp.max(part, axis=-1, keepdims=True) for part in scores]
        weights = [jnp.exp2((part - top) * scale) for part, top in zip(scores, tops)]
        totals = [jnp.sum(part, axis=-1, keepdims=True) for part in weights]
        blended = [
            jnp.dot(part.astype(jnp.bfloat16), tiles(1, cols), preferred_element_type=jnp.float32)
            for part, cols in zip(weights, doubles)
        ]
        for head, blend, total in zip(pairs, blended, totals):
            for side in range(2):
                cols = blocks[head + side]
                span = slice(side * rows, (side + 1) * rows)
                share = blend[span, side * head_dim : (side + 1) * head_dim] / total[span]
                state_ref[:, cols] = state[head + side] + mods[2:3, cols] * share

    layer(0)
    for slot in range(1, slots):
        pl.when(layer_count > slot)(functools.partial(layer, slot))

    if tick == 0:
        for head in range(heads):
            cols = slice(head * head_dim, (head + 1) * head_dim)
            out_ref[head * rows : (head + 1) * rows, :] = state_ref[:, cols].astype(out_ref.dtype)
        lanes = lax.broadcasted_iota(jnp.int32, (EXTRA, head_dim), 1)
        tail = jnp.where(lanes == 0, position, jnp.where(lanes == 1, step, 0))
        out_ref[heads * rows : heads * rows + EXTRA, :] = tail.astype(jnp.float32).astype(out_ref.dtype)
    else:
        out_ref[...] = state_ref[...].astype(out_ref.dtype)


def run_section(tick, start, rows, cycle_size, pipe, width, plan, patch, modulation, gains, own, other):
    heads = width // gains.shape[1]
    shape = (heads * rows + EXTRA, gains.shape[1]) if tick == 0 else (rows, width)
    return pl.pallas_call(
        functools.partial(section_kernel, tick, start, cycle_size, pipe),
        out_shape=pltpu.VMEM(shape, jnp.bfloat16),
        in_specs=[SMEM] + [VMEM] * 5,
        out_specs=VMEM,
        scratch_shapes=[pltpu.VMEM((rows, width), jnp.float32)],
        compiler_params=pltpu.CompilerParams(vmem_limit_bytes=16 << 20),
        cost_estimate=pl.CostEstimate(flops=400_000_000, bytes_accessed=8_000_000, transcendentals=800_000),
        name=f"section_{tick}_{start}",
    )(plan, pinned(patch), pinned(modulation), pinned(gains), pinned(own), pinned(other))


def place_kernel(starts, *refs):
    pieces, out_ref, sems = refs[: len(starts)], refs[-2], refs[-1]
    copies = [
        pltpu.make_async_copy(piece, out_ref.at[pl.ds(start, piece.shape[0])], sems.at[i])
        for i, (start, piece) in enumerate(zip(starts, pieces))
    ]
    for copy in copies:
        copy.start()
    for copy in copies:
        copy.wait()


def place(starts, pieces, tokens, into=None):
    width = pieces[0].shape[1]
    extra = [] if into is None else [pinned(into, pltpu.HBM)]
    return pl.pallas_call(
        functools.partial(place_kernel, starts),
        out_shape=pltpu.HBM((tokens, width), pieces[0].dtype),
        in_specs=[VMEM] * len(pieces) + [ANY] * len(extra),
        out_specs=ANY,
        scratch_shapes=[pltpu.SemaphoreType.DMA((len(pieces),))],
        input_output_aliases={} if into is None else {len(pieces): 0},
        compiler_params=pltpu.CompilerParams(vmem_limit_bytes=4 << 20),
        cost_estimate=pl.CostEstimate(flops=0, bytes_accessed=600_000, transcendentals=0),
        name=f"place_{starts[0]}",
    )(*(pinned(piece) for piece in pieces), *extra)


def per_device(
    patches, positions, timesteps, section_bounds, tile_neighbours, modulation, query_gain, stale_kv
):
    own_hbm = stale_kv[0]
    other = from_behind(own_hbm, "space", 1)
    cycle_size = lax.axis_size("segment")
    pipe = section_bounds.shape[0] - 1
    tokens, width = patches.shape[1:]
    plan, patch, mods, gains, own = stage(
        section_bounds, tile_neighbours.T, positions, timesteps, patches[0], modulation, query_gain, own_hbm
    )
    units = tokens // UNIT
    sizes = [UNIT * ((units + CHUNKS - 1 - chunk) // CHUNKS) for chunk in range(CHUNKS)]
    starts = [sum(sizes[:chunk]) for chunk in range(CHUNKS)]
    pieces = [patch] * CHUNKS
    for tick in range(TICKS):
        pieces = [
            from_behind(
                run_section(
                    tick, starts[chunk], sizes[chunk], cycle_size, pipe, width, plan, piece, mods, gains, own, other
                ),
                "segment",
                1,
            )
            for chunk, piece in enumerate(pieces)
        ]
    placed = place(starts[:-1], pieces[:-1], tokens)
    return place(starts[-1:], pieces[-1:], tokens, placed)[None]


def solution(mesh):
    placed = (
        P(("groups", "segment"), "space", None),
        P(("groups", "segment")),
        P(("groups", "segment")),
        P(),
        P(),
        P("groups", None, None, None),
        P(),
        P(("groups", "segment"), None, None, "space", None),
    )
    return jax.shard_map(
        per_device,
        mesh=mesh,
        in_specs=placed,
        out_specs=P(("groups", "segment"), "space", None),
        check_vma=False,
    )
```

```python
import functools
import math
import jax
import jax.numpy as jnp
from jax import lax
from jax.experimental import pallas as pl
from jax.experimental.pallas import tpu as pltpu
from jax.sharding import PartitionSpec as P

TICKS = 2
CHUNKS = 3
UNIT = 16
EPSILON = 1e-06
EXTRA = 8

SMEM = pl.BlockSpec(memory_space=pltpu.SMEM)
VMEM = pl.BlockSpec(memory_space=pltpu.VMEM)
ANY = pl.BlockSpec(memory_space=pl.ANY)


def from_behind(x, axis, by):
    devices = lax.axis_size(axis)
    return lax.ppermute(x, axis, [(i, (i + by) % devices) for i in range(devices)])


def pinned(x, space=pltpu.VMEM):
    return pltpu.with_memory_space_constraint(x, space)


def head_blocks(width, head_dim):
    return [slice(start, start + head_dim) for start in range(0, width, head_dim)]


def modulated_queries(state, mods, gain, blocks, width):
    middle = jnp.sum(sum(state[1:], state[0]), axis=-1, keepdims=True) / width
    centred = [part - middle for part in state]
    squares = [part * part for part in centred]
    spread = jnp.sum(sum(squares[1:], squares[0]), axis=-1, keepdims=True) / width
    sharp = lax.rsqrt(spread + EPSILON)
    shifted = [part * sharp * (1.0 + mods[1:2, cols]) + mods[0:1, cols] for part, cols in zip(centred, blocks)]
    powers = [jnp.mean(part * part, axis=-1, keepdims=True) for part in shifted]
    return [
        (part * lax.rsqrt(power + EPSILON) * gain).astype(jnp.bfloat16) for part, power in zip(shifted, powers)
    ]


def paired_queries(queries):
    blank = jnp.zeros_like(queries[0])
    return [
        jnp.concatenate(
            [
                jnp.concatenate([queries[head], blank], axis=1),
                jnp.concatenate([blank, queries[head + 1]], axis=1),
            ]
        )
        for head in range(0, len(queries), 2)
    ]


def transposed_dot(a, b):
    return lax.dot_general(a, b, (((1,), (1,)), ((), ())), preferred_element_type=jnp.float32)


def stage_kernel(
    bounds_hbm,
    neighbours_hbm,
    position_ref,
    step_ref,
    patch_ref,
    modulation_ref,
    gain_ref,
    own_ref,
    plan_ref,
    patch_out,
    modulation_out,
    gain_out,
    own_out,
    query_out,
    share_out,
    top_out,
    total_out,
    bounds_ref,
    neighbours_ref,
    sems,
):
    slots = own_ref.shape[0]
    far = sems.shape[0] - slots
    small = [
        pltpu.make_async_copy(source, target, sems.at[2 + slots + i])
        for i, (source, target) in enumerate(
            [
                (bounds_hbm, bounds_ref),
                (neighbours_hbm, neighbours_ref),
            ]
        )
    ]
    copies = [
        pltpu.make_async_copy(patch_ref, patch_out, sems.at[0]),
        pltpu.make_async_copy(gain_ref, gain_out, sems.at[1]),
    ]
    slabs = [pltpu.make_async_copy(own_ref.at[slot], own_out.at[slot], sems.at[far + slot]) for slot in range(slots)]
    for copy in small + copies + slabs:
        copy.start()
    for copy in small:
        copy.wait()
    pipe = bounds_ref.shape[0] - 1
    layers = gain_ref.shape[0]
    device = lax.axis_index("segment")
    space = lax.axis_index("space")
    section = lax.rem(device, pipe)
    first_layer = bounds_ref[section]
    for slot in range(slots):
        layer_now = jnp.minimum(first_layer + slot, layers - 1)
        copy = pltpu.make_async_copy(modulation_ref.at[:, layer_now], modulation_out.at[slot], sems.at[2 + slot])
        copy.start()
        copies.append(copy)
    slab = neighbours_ref.shape[1] // 2
    plan_ref[0] = first_layer
    plan_ref[1] = bounds_ref[section + 1] - first_layer
    plan_ref[2] = position_ref[0]
    plan_ref[3] = step_ref[0]
    for place in range(slab):
        plan_ref[4 + place] = lax.rem(neighbours_ref[0, space * slab + place], slab)
        plan_ref[4 + slab + place] = lax.rem(neighbours_ref[1, space * slab + place], slab)
    for copy in copies:
        copy.wait()
    slabs[0].wait()

    tile = own_ref.shape[2] // slab
    rows, width = patch_ref.shape
    head_dim = gain_ref.shape[1]
    blocks = head_blocks(width, head_dim)
    own_row = pl.multiple_of(plan_ref[4 + position_ref[0]] * tile, tile)
    scale = head_dim ** -0.5 * math.log2(math.e)
    mods = modulation_out[0, step_ref[0]].astype(jnp.float32)
    gain = gain_out[pl.ds(first_layer, 1), :]
    state = [patch_out[:, cols].astype(jnp.float32) for cols in blocks]
    queries = modulated_queries(state, mods, gain, blocks, width)
    scores = [
        transposed_dot(query, own_out[0, 0, pl.ds(own_row, tile), cols]) for query, cols in zip(queries, blocks)
    ]
    tops = [jnp.max(part, axis=-1, keepdims=True) for part in scores]
    weights = [jnp.exp2((part - top) * scale) for part, top in zip(scores, tops)]
    totals = [jnp.sum(part, axis=-1, keepdims=True) for part in weights]
    shares = [
        jnp.dot(
            part.astype(jnp.bfloat16),
            own_out[0, 1, pl.ds(own_row, tile), cols],
            preferred_element_type=jnp.float32,
        )
        for part, cols in zip(weights, blocks)
    ]
    for head, cols in enumerate(blocks):
        query_out[:, cols] = queries[head]
        share_out[:, cols] = shares[head]
        top_out[:, cols] = jnp.broadcast_to(tops[head], shares[head].shape)
        total_out[:, cols] = jnp.broadcast_to(totals[head], shares[head].shape)
    for copy in slabs[1:]:
        copy.wait()


def stage(bounds, neighbours, position, step, patch, modulation, gains, own):
    slots = own.shape[0]
    plan_size = 4 + neighbours.shape[1]
    return pl.pallas_call(
        stage_kernel,
        out_shape=(
            pltpu.SMEM((plan_size,), jnp.int32),
            pltpu.VMEM(patch.shape, patch.dtype),
            pltpu.VMEM((slots, modulation.shape[0]) + modulation.shape[2:], modulation.dtype),
            pltpu.VMEM(gains.shape, gains.dtype),
            pltpu.VMEM(own.shape, own.dtype),
            pltpu.VMEM(patch.shape, jnp.bfloat16),
            pltpu.VMEM(patch.shape, jnp.float32),
            pltpu.VMEM(patch.shape, jnp.float32),
            pltpu.VMEM(patch.shape, jnp.float32),
        ),
        in_specs=[ANY] * 2 + [SMEM] * 2 + [ANY] * 4,
        out_specs=(SMEM,) + (VMEM,) * 8,
        scratch_shapes=[pltpu.SMEM(x.shape, x.dtype) for x in (bounds, neighbours)]
        + [pltpu.SemaphoreType.DMA((4 + 2 * slots,))],
        compiler_params=pltpu.CompilerParams(vmem_limit_bytes=16 << 20),
        cost_estimate=pl.CostEstimate(flops=100_000_000, bytes_accessed=8_000_000, transcendentals=200_000),
        name="stage",
    )(
        pinned(bounds, pltpu.HBM),
        pinned(neighbours, pltpu.HBM),
        position,
        step,
        *(pinned(x, pltpu.HBM) for x in (patch, modulation, gains, own)),
    )


def section_kernel(
    tick,
    start,
    cycle_size,
    pipe,
    plan_ref,
    patch_ref,
    modulation_ref,
    gain_ref,
    own_ref,
    other_ref,
    *refs,
):
    half, (out_ref, state_ref) = refs[:-2], refs[-2:]
    rows, width = state_ref.shape
    layers, head_dim = gain_ref.shape
    heads = width // head_dim
    slots = own_ref.shape[0]
    slab = (plan_ref.shape[0] - 4) // 2
    tile = own_ref.shape[2] // slab
    device = lax.axis_index("segment")
    root = lax.rem(device - tick + cycle_size, cycle_size)
    if tick == 0:
        position = plan_ref[2]
        step = plan_ref[3]
    else:
        tail = patch_ref[heads * rows : heads * rows + EXTRA, :].astype(jnp.float32)
        lanes = lax.broadcasted_iota(jnp.int32, tail.shape, 1)
        position = jnp.max(jnp.where(lanes == 0, tail, 0.0)).astype(jnp.int32)
        step = jnp.max(jnp.where(lanes == 1, tail, 0.0)).astype(jnp.int32)
    row = step + jnp.where(lax.rem(root, pipe) + tick >= pipe, 1, 0)
    first_layer = plan_ref[0]
    layer_count = plan_ref[1]
    own_row = pl.multiple_of(plan_ref[4 + position] * tile, tile)
    other_row = pl.multiple_of(plan_ref[4 + slab + position] * tile, tile)
    scale = head_dim ** -0.5 * math.log2(math.e)

    for head in range(heads):
        cols = slice(head * head_dim, (head + 1) * head_dim)
        if tick == 0:
            state_ref[:, cols] = patch_ref[start : start + rows, cols].astype(jnp.float32)
        else:
            state_ref[:, cols] = patch_ref[head * rows : (head + 1) * rows, :].astype(jnp.float32)

    def layer(slot):
        layer_now = jnp.minimum(first_layer + slot, layers - 1)
        mods = modulation_ref[slot, row].astype(jnp.float32)
        gain = gain_ref[pl.ds(layer_now, 1), :]
        blocks = head_blocks(width, head_dim)
        pairs = range(0, heads, 2)
        doubles = head_blocks(width, 2 * head_dim)
        split = tick == 0 and slot == 0

        def tiles(kind, cols):
            theirs = other_ref[slot, kind, pl.ds(other_row, tile), cols]
            if split:
                return theirs
            return jnp.concatenate([own_ref[slot, kind, pl.ds(own_row, tile), cols], theirs])

        state = [state_ref[:, cols] for cols in blocks]
        if split:
            query_ref, share_ref, top_ref, total_ref = half
            window = slice(start, start + rows)
            queries = [query_ref[window, cols] for cols in blocks]
        else:
            queries = modulated_queries(state, mods, gain, blocks, width)
        paired = paired_queries(queries)
        scores = [transposed_dot(query, tiles(0, cols)) for query, cols in zip(paired, doubles)]
        tops = [jnp.max(part, axis=-1, keepdims=True) for part in scores]
        if split:
            own_tops = [
                jnp.concatenate([top_ref[window, blocks[head]], top_ref[window, blocks[head + 1]]])
                for head in pairs
            ]
            tops = [jnp.maximum(top, own_top) for top, own_top in zip(tops, own_tops)]
            fades = [jnp.exp2((own_top - top) * scale) for top, own_top in zip(tops, own_tops)]
        weights = [jnp.exp2((part - top) * scale) for part, top in zip(scores, tops)]
        totals = [jnp.sum(part, axis=-1, keepdims=True) for part in weights]
        blended = [
            jnp.dot(part.astype(jnp.bfloat16), tiles(1, cols), preferred_element_type=jnp.float32)
            for part, cols in zip(weights, doubles)
        ]
        for pair, (blend, total) in enumerate(zip(blended, totals)):
            for side in range(2):
                head = 2 * pair + side
                cols = blocks[head]
                span = slice(side * rows, (side + 1) * rows)
                share = blend[span, side * head_dim : (side + 1) * head_dim]
                whole = total[span]
                if split:
                    fade = fades[pair][span]
                    share = share + fade * share_ref[window, cols]
                    whole = whole + fade * total_ref[window, cols]
                state_ref[:, cols] = state[head] + mods[2:3, cols] * (share / whole)

    layer(0)
    for slot in range(1, slots):
        pl.when(layer_count > slot)(functools.partial(layer, slot))

    if tick == 0:
        for head in range(heads):
            cols = slice(head * head_dim, (head + 1) * head_dim)
            out_ref[head * rows : (head + 1) * rows, :] = state_ref[:, cols].astype(out_ref.dtype)
        lanes = lax.broadcasted_iota(jnp.int32, (EXTRA, head_dim), 1)
        tail = jnp.where(lanes == 0, position, jnp.where(lanes == 1, step, 0))
        out_ref[heads * rows : heads * rows + EXTRA, :] = tail.astype(jnp.float32).astype(out_ref.dtype)
    else:
        out_ref[...] = state_ref[...].astype(out_ref.dtype)


def run_section(tick, start, rows, cycle_size, pipe, width, plan, patch, modulation, gains, own, other, half):
    heads = width // gains.shape[1]
    shape = (heads * rows + EXTRA, gains.shape[1]) if tick == 0 else (rows, width)
    return pl.pallas_call(
        functools.partial(section_kernel, tick, start, cycle_size, pipe),
        out_shape=pltpu.VMEM(shape, jnp.bfloat16),
        in_specs=[SMEM] + [VMEM] * (5 + len(half)),
        out_specs=VMEM,
        scratch_shapes=[pltpu.VMEM((rows, width), jnp.float32)],
        compiler_params=pltpu.CompilerParams(vmem_limit_bytes=16 << 20),
        cost_estimate=pl.CostEstimate(flops=400_000_000, bytes_accessed=8_000_000, transcendentals=800_000),
        name=f"section_{tick}_{start}",
    )(plan, pinned(patch), pinned(modulation), pinned(gains), pinned(own), pinned(other), *(pinned(x) for x in half))


def place_kernel(starts, *refs):
    pieces, out_ref, sems = refs[: len(starts)], refs[-2], refs[-1]
    copies = [
        pltpu.make_async_copy(piece, out_ref.at[pl.ds(start, piece.shape[0])], sems.at[i])
        for i, (start, piece) in enumerate(zip(starts, pieces))
    ]
    for copy in copies:
        copy.start()
    for copy in copies:
        copy.wait()


def place(starts, pieces, tokens, into=None):
    width = pieces[0].shape[1]
    extra = [] if into is None else [pinned(into, pltpu.HBM)]
    return pl.pallas_call(
        functools.partial(place_kernel, starts),
        out_shape=pltpu.HBM((tokens, width), pieces[0].dtype),
        in_specs=[VMEM] * len(pieces) + [ANY] * len(extra),
        out_specs=ANY,
        scratch_shapes=[pltpu.SemaphoreType.DMA((len(pieces),))],
        input_output_aliases={} if into is None else {len(pieces): 0},
        compiler_params=pltpu.CompilerParams(vmem_limit_bytes=4 << 20),
        cost_estimate=pl.CostEstimate(flops=0, bytes_accessed=600_000, transcendentals=0),
        name=f"place_{starts[0]}",
    )(*(pinned(piece) for piece in pieces), *extra)


def per_device(
    patches, positions, timesteps, section_bounds, tile_neighbours, modulation, query_gain, stale_kv
):
    own_hbm = stale_kv[0]
    other = from_behind(own_hbm, "space", 1)
    cycle_size = lax.axis_size("segment")
    pipe = section_bounds.shape[0] - 1
    tokens, width = patches.shape[1:]
    plan, patch, mods, gains, own, *half = stage(
        section_bounds, tile_neighbours.T, positions, timesteps, patches[0], modulation, query_gain, own_hbm
    )
    units = tokens // UNIT
    sizes = [UNIT * ((units + CHUNKS - 1 - chunk) // CHUNKS) for chunk in range(CHUNKS)]
    starts = [sum(sizes[:chunk]) for chunk in range(CHUNKS)]
    pieces = [patch] * CHUNKS
    for tick in range(TICKS):
        pieces = [
            from_behind(
                run_section(
                    tick, starts[chunk], sizes[chunk], cycle_size, pipe, width, plan, piece, mods, gains, own, other, half if tick == 0 else []
                ),
                "segment",
                1,
            )
            for chunk, piece in enumerate(pieces)
        ]
    placed = place(starts[:-1], pieces[:-1], tokens)
    return place(starts[-1:], pieces[-1:], tokens, placed)[None]


def solution(mesh):
    placed = (
        P(("groups", "segment"), "space", None),
        P(("groups", "segment")),
        P(("groups", "segment")),
        P(),
        P(),
        P("groups", None, None, None),
        P(),
        P(("groups", "segment"), None, None, "space", None),
    )
    return jax.shard_map(
        per_device,
        mesh=mesh,
        in_specs=placed,
        out_specs=P(("groups", "segment"), "space", None),
        check_vma=False,
    )
```

```python
import functools
import math
import jax
import jax.numpy as jnp
from jax import lax
from jax.experimental import pallas as pl
from jax.experimental.pallas import tpu as pltpu
from jax.sharding import PartitionSpec as P

TICKS = 2
CHUNKS = 3
UNIT = 16
EPSILON = 1e-06
EXTRA = 8

SMEM = pl.BlockSpec(memory_space=pltpu.SMEM)
VMEM = pl.BlockSpec(memory_space=pltpu.VMEM)
ANY = pl.BlockSpec(memory_space=pl.ANY)


def from_behind(x, axis, by):
    devices = lax.axis_size(axis)
    return lax.ppermute(x, axis, [(i, (i + by) % devices) for i in range(devices)])


def pinned(x, space=pltpu.VMEM):
    return pltpu.with_memory_space_constraint(x, space)


def head_blocks(width, head_dim):
    return [slice(start, start + head_dim) for start in range(0, width, head_dim)]


def modulated_queries(state, mods, gain, blocks, width):
    middle = jnp.sum(sum(state[1:], state[0]), axis=-1, keepdims=True) / width
    centred = [part - middle for part in state]
    squares = [part * part for part in centred]
    spread = jnp.sum(sum(squares[1:], squares[0]), axis=-1, keepdims=True) / width
    sharp = lax.rsqrt(spread + EPSILON)
    shifted = [part * sharp * (1.0 + mods[1:2, cols]) + mods[0:1, cols] for part, cols in zip(centred, blocks)]
    powers = [jnp.mean(part * part, axis=-1, keepdims=True) for part in shifted]
    return [
        (part * lax.rsqrt(power + EPSILON) * gain).astype(jnp.bfloat16) for part, power in zip(shifted, powers)
    ]


def paired_queries(queries):
    blank = jnp.zeros_like(queries[0])
    return [
        jnp.concatenate(
            [
                jnp.concatenate([queries[head], blank], axis=1),
                jnp.concatenate([blank, queries[head + 1]], axis=1),
            ]
        )
        for head in range(0, len(queries), 2)
    ]


def transposed_dot(a, b):
    return lax.dot_general(a, b, (((1,), (1,)), ((), ())), preferred_element_type=jnp.float32)


def stage_kernel(
    bounds_hbm,
    neighbours_hbm,
    position_ref,
    step_ref,
    patch_ref,
    modulation_ref,
    gain_ref,
    own_ref,
    plan_ref,
    patch_out,
    modulation_out,
    gain_out,
    own_out,
    query_out,
    score_out,
    bounds_ref,
    neighbours_ref,
    sems,
):
    slots = own_ref.shape[0]
    far = sems.shape[0] - slots
    small = [
        pltpu.make_async_copy(source, target, sems.at[2 + slots + i])
        for i, (source, target) in enumerate(
            [
                (bounds_hbm, bounds_ref),
                (neighbours_hbm, neighbours_ref),
            ]
        )
    ]
    copies = [
        pltpu.make_async_copy(patch_ref, patch_out, sems.at[0]),
        pltpu.make_async_copy(gain_ref, gain_out, sems.at[1]),
    ]
    slabs = [pltpu.make_async_copy(own_ref.at[slot], own_out.at[slot], sems.at[far + slot]) for slot in range(slots)]
    for copy in small + copies + slabs:
        copy.start()
    for copy in small:
        copy.wait()
    pipe = bounds_ref.shape[0] - 1
    layers = gain_ref.shape[0]
    device = lax.axis_index("segment")
    space = lax.axis_index("space")
    section = lax.rem(device, pipe)
    first_layer = bounds_ref[section]
    for slot in range(slots):
        layer_now = jnp.minimum(first_layer + slot, layers - 1)
        copy = pltpu.make_async_copy(modulation_ref.at[:, layer_now], modulation_out.at[slot], sems.at[2 + slot])
        copy.start()
        copies.append(copy)
    slab = neighbours_ref.shape[1] // 2
    plan_ref[0] = first_layer
    plan_ref[1] = bounds_ref[section + 1] - first_layer
    plan_ref[2] = position_ref[0]
    plan_ref[3] = step_ref[0]
    for place in range(slab):
        plan_ref[4 + place] = lax.rem(neighbours_ref[0, space * slab + place], slab)
        plan_ref[4 + slab + place] = lax.rem(neighbours_ref[1, space * slab + place], slab)
    for copy in copies:
        copy.wait()
    slabs[0].wait()

    tile = own_ref.shape[2] // slab
    rows, width = patch_ref.shape
    head_dim = gain_ref.shape[1]
    blocks = head_blocks(width, head_dim)
    own_row = pl.multiple_of(plan_ref[4 + position_ref[0]] * tile, tile)
    mods = modulation_out[0, step_ref[0]].astype(jnp.float32)
    gain = gain_out[pl.ds(first_layer, 1), :]
    state = [patch_out[:, cols].astype(jnp.float32) for cols in blocks]
    queries = modulated_queries(state, mods, gain, blocks, width)
    scores = [
        transposed_dot(query, own_out[0, 0, pl.ds(own_row, tile), cols]) for query, cols in zip(queries, blocks)
    ]
    for query, part, cols in zip(queries, scores, blocks):
        query_out[:, cols] = query
        score_out[:, cols] = part
    for copy in slabs[1:]:
        copy.wait()


def stage(bounds, neighbours, position, step, patch, modulation, gains, own):
    slots = own.shape[0]
    plan_size = 4 + neighbours.shape[1]
    return pl.pallas_call(
        stage_kernel,
        out_shape=(
            pltpu.SMEM((plan_size,), jnp.int32),
            pltpu.VMEM(patch.shape, patch.dtype),
            pltpu.VMEM((slots, modulation.shape[0]) + modulation.shape[2:], modulation.dtype),
            pltpu.VMEM(gains.shape, gains.dtype),
            pltpu.VMEM(own.shape, own.dtype),
            pltpu.VMEM(patch.shape, jnp.bfloat16),
            pltpu.VMEM(patch.shape, jnp.float32),
        ),
        in_specs=[ANY] * 2 + [SMEM] * 2 + [ANY] * 4,
        out_specs=(SMEM,) + (VMEM,) * 6,
        scratch_shapes=[pltpu.SMEM(x.shape, x.dtype) for x in (bounds, neighbours)]
        + [pltpu.SemaphoreType.DMA((4 + 2 * slots,))],
        compiler_params=pltpu.CompilerParams(vmem_limit_bytes=16 << 20),
        cost_estimate=pl.CostEstimate(flops=100_000_000, bytes_accessed=8_000_000, transcendentals=200_000),
        name="stage",
    )(
        pinned(bounds, pltpu.HBM),
        pinned(neighbours, pltpu.HBM),
        position,
        step,
        *(pinned(x, pltpu.HBM) for x in (patch, modulation, gains, own)),
    )


def section_kernel(
    tick,
    start,
    cycle_size,
    pipe,
    plan_ref,
    patch_ref,
    modulation_ref,
    gain_ref,
    own_ref,
    other_ref,
    *refs,
):
    half, (out_ref, state_ref) = refs[:-2], refs[-2:]
    rows, width = state_ref.shape
    layers, head_dim = gain_ref.shape
    heads = width // head_dim
    slots = own_ref.shape[0]
    slab = (plan_ref.shape[0] - 4) // 2
    tile = own_ref.shape[2] // slab
    device = lax.axis_index("segment")
    root = lax.rem(device - tick + cycle_size, cycle_size)
    if tick == 0:
        position = plan_ref[2]
        step = plan_ref[3]
    else:
        tail = patch_ref[heads * rows : heads * rows + EXTRA, :].astype(jnp.float32)
        lanes = lax.broadcasted_iota(jnp.int32, tail.shape, 1)
        position = jnp.max(jnp.where(lanes == 0, tail, 0.0)).astype(jnp.int32)
        step = jnp.max(jnp.where(lanes == 1, tail, 0.0)).astype(jnp.int32)
    row = step + jnp.where(lax.rem(root, pipe) + tick >= pipe, 1, 0)
    first_layer = plan_ref[0]
    layer_count = plan_ref[1]
    own_row = pl.multiple_of(plan_ref[4 + position] * tile, tile)
    other_row = pl.multiple_of(plan_ref[4 + slab + position] * tile, tile)
    scale = head_dim ** -0.5 * math.log2(math.e)

    for head in range(heads):
        cols = slice(head * head_dim, (head + 1) * head_dim)
        if tick == 0:
            state_ref[:, cols] = patch_ref[start : start + rows, cols].astype(jnp.float32)
        else:
            state_ref[:, cols] = patch_ref[head * rows : (head + 1) * rows, :].astype(jnp.float32)

    def layer(slot):
        layer_now = jnp.minimum(first_layer + slot, layers - 1)
        mods = modulation_ref[slot, row].astype(jnp.float32)
        gain = gain_ref[pl.ds(layer_now, 1), :]
        blocks = head_blocks(width, head_dim)
        pairs = range(0, heads, 2)
        doubles = head_blocks(width, 2 * head_dim)
        split = tick == 0 and slot == 0

        def tiles(kind, cols):
            theirs = other_ref[slot, kind, pl.ds(other_row, tile), cols]
            if split and kind == 0:
                return theirs
            return jnp.concatenate([own_ref[slot, kind, pl.ds(own_row, tile), cols], theirs])

        state = [state_ref[:, cols] for cols in blocks]
        if split:
            query_ref, score_ref = half
            window = slice(start, start + rows)
            queries = [query_ref[window, cols] for cols in blocks]
        else:
            queries = modulated_queries(state, mods, gain, blocks, width)
        paired = paired_queries(queries)
        scores = [transposed_dot(query, tiles(0, cols)) for query, cols in zip(paired, doubles)]
        if split:
            scores = [
                jnp.concatenate(
                    [jnp.concatenate([score_ref[window, blocks[head]], score_ref[window, blocks[head + 1]]]), part],
                    axis=1,
                )
                for head, part in zip(pairs, scores)
            ]
        tops = [jnp.max(part, axis=-1, keepdims=True) for part in scores]
        weights = [jnp.exp2((part - top) * scale) for part, top in zip(scores, tops)]
        totals = [jnp.sum(part, axis=-1, keepdims=True) for part in weights]
        blended = [
            jnp.dot(part.astype(jnp.bfloat16), tiles(1, cols), preferred_element_type=jnp.float32)
            for part, cols in zip(weights, doubles)
        ]
        for pair, (blend, total) in enumerate(zip(blended, totals)):
            for side in range(2):
                head = 2 * pair + side
                cols = blocks[head]
                span = slice(side * rows, (side + 1) * rows)
                share = blend[span, side * head_dim : (side + 1) * head_dim] / total[span]
                state_ref[:, cols] = state[head] + mods[2:3, cols] * share

    layer(0)
    for slot in range(1, slots):
        pl.when(layer_count > slot)(functools.partial(layer, slot))

    if tick == 0:
        for head in range(heads):
            cols = slice(head * head_dim, (head + 1) * head_dim)
            out_ref[head * rows : (head + 1) * rows, :] = state_ref[:, cols].astype(out_ref.dtype)
        lanes = lax.broadcasted_iota(jnp.int32, (EXTRA, head_dim), 1)
        tail = jnp.where(lanes == 0, position, jnp.where(lanes == 1, step, 0))
        out_ref[heads * rows : heads * rows + EXTRA, :] = tail.astype(jnp.float32).astype(out_ref.dtype)
    else:
        out_ref[...] = state_ref[...].astype(out_ref.dtype)


def run_section(tick, start, rows, cycle_size, pipe, width, plan, patch, modulation, gains, own, other, half):
    heads = width // gains.shape[1]
    shape = (heads * rows + EXTRA, gains.shape[1]) if tick == 0 else (rows, width)
    return pl.pallas_call(
        functools.partial(section_kernel, tick, start, cycle_size, pipe),
        out_shape=pltpu.VMEM(shape, jnp.bfloat16),
        in_specs=[SMEM] + [VMEM] * (5 + len(half)),
        out_specs=VMEM,
        scratch_shapes=[pltpu.VMEM((rows, width), jnp.float32)],
        compiler_params=pltpu.CompilerParams(vmem_limit_bytes=16 << 20),
        cost_estimate=pl.CostEstimate(flops=400_000_000, bytes_accessed=8_000_000, transcendentals=800_000),
        name=f"section_{tick}_{start}",
    )(plan, pinned(patch), pinned(modulation), pinned(gains), pinned(own), pinned(other), *(pinned(x) for x in half))


def place_kernel(starts, *refs):
    pieces, out_ref, sems = refs[: len(starts)], refs[-2], refs[-1]
    copies = [
        pltpu.make_async_copy(piece, out_ref.at[pl.ds(start, piece.shape[0])], sems.at[i])
        for i, (start, piece) in enumerate(zip(starts, pieces))
    ]
    for copy in copies:
        copy.start()
    for copy in copies:
        copy.wait()


def place(starts, pieces, tokens, into=None):
    width = pieces[0].shape[1]
    extra = [] if into is None else [pinned(into, pltpu.HBM)]
    return pl.pallas_call(
        functools.partial(place_kernel, starts),
        out_shape=pltpu.HBM((tokens, width), pieces[0].dtype),
        in_specs=[VMEM] * len(pieces) + [ANY] * len(extra),
        out_specs=ANY,
        scratch_shapes=[pltpu.SemaphoreType.DMA((len(pieces),))],
        input_output_aliases={} if into is None else {len(pieces): 0},
        compiler_params=pltpu.CompilerParams(vmem_limit_bytes=4 << 20),
        cost_estimate=pl.CostEstimate(flops=0, bytes_accessed=600_000, transcendentals=0),
        name=f"place_{starts[0]}",
    )(*(pinned(piece) for piece in pieces), *extra)


def per_device(
    patches, positions, timesteps, section_bounds, tile_neighbours, modulation, query_gain, stale_kv
):
    own_hbm = stale_kv[0]
    other = from_behind(own_hbm, "space", 1)
    cycle_size = lax.axis_size("segment")
    pipe = section_bounds.shape[0] - 1
    tokens, width = patches.shape[1:]
    plan, patch, mods, gains, own, *half = stage(
        section_bounds, tile_neighbours.T, positions, timesteps, patches[0], modulation, query_gain, own_hbm
    )
    units = tokens // UNIT
    sizes = [UNIT * ((units + CHUNKS - 1 - chunk) // CHUNKS) for chunk in range(CHUNKS)]
    starts = [sum(sizes[:chunk]) for chunk in range(CHUNKS)]
    pieces = [patch] * CHUNKS
    for tick in range(TICKS):
        pieces = [
            from_behind(
                run_section(
                    tick, starts[chunk], sizes[chunk], cycle_size, pipe, width, plan, piece, mods, gains, own, other, half if tick == 0 else []
                ),
                "segment",
                1,
            )
            for chunk, piece in enumerate(pieces)
        ]
    placed = place(starts[:-1], pieces[:-1], tokens)
    return place(starts[-1:], pieces[-1:], tokens, placed)[None]


def solution(mesh):
    placed = (
        P(("groups", "segment"), "space", None),
        P(("groups", "segment")),
        P(("groups", "segment")),
        P(),
        P(),
        P("groups", None, None, None),
        P(),
        P(("groups", "segment"), None, None, "space", None),
    )
    return jax.shard_map(
        per_device,
        mesh=mesh,
        in_specs=placed,
        out_specs=P(("groups", "segment"), "space", None),
        check_vma=False,
    )
```
